512 devices in a mesh: gx: 16 (over z), gy: 32 (over x, y, core).
Axes of the slice: x: 4, y: 4, z: 16, core: 2. Of those that a mesh axis runs over, the one named last changes fastest.
Arguments:
- labels: int32 [64, 256, 128], P('gx', 'gy'), may hold values from 0 to 16, as said below
- layer_index: int32 [128], replicated, may hold values from 0 to 7
- layer_eps: float32 [8], replicated, may hold values from 1 to 12
Outputs:
- solution_block: float32 [16, 64, 256, 128], P(None, 'gx', 'gy')
- residual_block: float32 [16, 64, 256, 128], P(None, 'gx', 'gy')
The draws below stay inside these ranges and needn't reach their ends.
Inputs may be any that keep to these rules, and one draw needn't show every extreme that they name: `labels`: 0 marks a dielectric cell; k marks a cell of conductor k.
All inputs are finite; a program needn't handle non-finite values.
Results may differ from the reference program's by a relative error of at most 0.0003.
Values sent between devices are 32-bit elements; how exact they have to be, the bound alone decides.
No kernel may reach another device: no remote copies, remote signals or barrier semaphores. Data moves between devices by JAX's collectives and lax.ppermute only.
A program may use at most 64 MiB of HBM per device.

```python
import math
import jax
import jax.numpy as jnp
from jax import lax

K = 16
LAYERS = 8
NZ = 128
ITERS = 3
NX = 64
NY = 256


def draw_labels(key, part):
    raw = jax.random.randint(key, (NX, NY, NZ), 0, 10 * K, dtype=jnp.int32)
    return jnp.where(raw < K, raw + 1, 0).astype(jnp.int32)


def plant(array, own_key, low, largest):
    place = [jax.random.randint(jax.random.fold_in(own_key, axis), (), 0, length) for axis, length in enumerate(array.shape)]
    longest = array.shape.index(max(array.shape))
    next_to = place[:longest] + [(place[longest] + 1) % array.shape[longest]] + place[longest + 1:]
    return array.at[tuple(place)].set(low).at[tuple(next_to)].set(largest)


def setup_inputs(seed: int = 0) -> dict:
    seeds = jax.random.split(jax.random.key(seed), 4)
    labels = draw_labels(jax.random.fold_in(seeds[3], 71), 0)
    layer_index = plant(jax.random.randint(seeds[1], (NZ,), 0, LAYERS), jax.random.fold_in(seeds[1], 1), 0, LAYERS - 1).astype(jnp.int32)
    layer_eps = jnp.clip(jnp.exp(jax.random.uniform(seeds[2], (LAYERS,), jnp.float32, math.log(1.0), math.log(12.0))), 1.0, 12.0)
    return {"labels": labels, "layer_index": layer_index, "layer_eps": layer_eps}


def coefficients(layer_index, layer_eps):
    eps_plane = layer_eps[layer_index]
    middle = 0.5 * (eps_plane[1:] + eps_plane[:-1])
    c_down = jnp.concatenate([eps_plane[:1], middle])
    c_up = jnp.concatenate([middle, eps_plane[-1:]])
    diagonal = 4.0 * eps_plane + c_down + c_up
    return (eps_plane, c_down, c_up, diagonal)

def laplace(padded, coeffs):
    eps_plane, c_down, c_up, diagonal = coeffs
    field = padded[:, 1:-1, 1:-1]
    lateral = padded[:, 2:, 1:-1] + padded[:, :-2, 1:-1] + padded[:, 1:-1, 2:] + padded[:, 1:-1, :-2]
    below = jnp.pad(field[..., :-1], ((0, 0), (0, 0), (0, 0), (1, 0)))
    above = jnp.pad(field[..., 1:], ((0, 0), (0, 0), (0, 0), (0, 1)))
    return diagonal * field - eps_plane * lateral - c_down * below - c_up * above

def pad_lateral(field):
    return jnp.pad(field, ((0, 0), (1, 1), (1, 1), (0, 0)))

def gram_of(left, right):
    count = left.shape[0]
    return jnp.dot(left.reshape(count, -1).astype(jnp.float32), right.reshape(count, -1).T.astype(jnp.float32), precision=lax.Precision.HIGHEST, preferred_element_type=jnp.float32)

def combine_rows(coef, field):
    count = field.shape[0]
    return jnp.dot(coef.astype(jnp.float32), field.reshape(count, -1).astype(jnp.float32), precision=lax.Precision.HIGHEST, preferred_element_type=jnp.float32).reshape(field.shape)

def lower_inverse(factor):
    count = factor.shape[0]
    inverse = jnp.zeros((count, count), jnp.float32)
    unit = jnp.eye(count, dtype=jnp.float32)
    for row in range(count):
        partial_row = unit[row] - jnp.dot(factor[row], inverse, precision=lax.Precision.HIGHEST)
        inverse = inverse.at[row].set(partial_row / factor[row, row])
    return inverse

def reference(labels, layer_index, layer_eps):
    coeffs = coefficients(layer_index, layer_eps)
    free = (labels == 0).astype(jnp.float32)
    conductor_ids = jnp.arange(1, K + 1, dtype=jnp.int32)
    excitation = (labels[None] == conductor_ids[:, None, None, None]).astype(jnp.float32)
    right_side = -free * laplace(pad_lateral(excitation), coeffs)
    inverse_diag = free / coeffs[3]
    solution = jnp.zeros_like(right_side)
    residual = right_side
    prev_search = None
    prev_image = None
    for step in range(ITERS):
        precond = inverse_diag * residual
        if step == 0:
            search = precond
        else:
            beta = gram_of(prev_image, precond)
            search = precond - combine_rows(beta.T, prev_search)
        image = free * laplace(pad_lateral(search), coeffs)
        factor = jnp.linalg.cholesky(gram_of(search, image))
        inverse = lower_inverse(factor)
        prev_search = combine_rows(inverse, search)
        prev_image = combine_rows(inverse, image)
        alpha = gram_of(prev_search, residual)
        solution = solution + combine_rows(alpha.T, prev_search)
        residual = residual - combine_rows(alpha.T, prev_image)
    return (solution, residual)
```

```python
import functools

import jax
import jax.numpy as jnp
from jax import lax
from jax.experimental import pallas as pl
from jax.experimental.pallas import tpu as pltpu
from jax.sharding import PartitionSpec as P

K = 16
DEPTH = 4
HIGHEST = lax.Precision.HIGHEST


def plane_coefficients(index_ref, eps_ref):
    index = index_ref[...]
    eps = jnp.zeros(index.shape, jnp.float32)
    for layer in range(eps_ref.shape[0]):
        eps = jnp.where(index == layer, eps_ref[layer], eps)
    count = index.shape[-1]
    lane = lax.broadcasted_iota(jnp.int32, index.shape, 1)
    down = jnp.where(lane == 0, eps, 0.5 * (eps + pltpu.roll(eps, 1, 1)))
    up = jnp.where(lane == count - 1, eps, 0.5 * (eps + pltpu.roll(eps, count - 1, 1)))
    diag = 4.0 * eps + down + up
    return eps, down, up, diag, lane


def basis_kernel(place_ref, mid_ref, low_ref, high_ref, index_ref, eps_ref, basis_ref, moments_ref, lab, b0, b1, b2, b3, scaled):
    nx, wide, nz = mid_ref.shape
    ny = wide - 2 * DEPTH
    eps, down, up, diag, lane = plane_coefficients(index_ref, eps_ref)
    inverse = 1.0 / diag
    shape = (K, nz)
    lateral_c = jnp.broadcast_to(eps * inverse, shape)
    below_c = jnp.broadcast_to(jnp.where(lane == 0, 0.0, down * inverse), shape)
    above_c = jnp.broadcast_to(jnp.where(lane == nz - 1, 0.0, up * inverse), shape)
    row = lax.broadcasted_iota(jnp.int32, shape, 0) + 1
    for part, ref in enumerate((low_ref, mid_ref, high_ref)):
        inside = place_ref[part] > 0
        for x in range(nx):
            for y in range(wide):
                label = jnp.broadcast_to(ref[x, y : y + 1, :], shape)
                label = jnp.where(inside, label, -1)
                lab[part * nx + x, y] = label[:8]
                b0[part * nx + x, y] = (label == row).astype(jnp.float32)
    rows, cols = 3 * nx, wide
    bufs = (b0, b1, b2, b3, b0)
    for level in range(1, DEPTH + 1):
        source, target = bufs[level - 1], bufs[level]
        rows, cols = rows - 2, cols - 2

        def one_row(x, _, source=source, target=target, cols=cols, level=level):
            for y in range(cols):
                centre = source[x + 1, y + 1]
                lateral = (source[x, y + 1] + source[x + 2, y + 1]) + (source[x + 1, y] + source[x + 1, y + 2])
                value = (
                    lateral_c * lateral
                    + below_c * pltpu.roll(centre, 1, 1)
                    + above_c * pltpu.roll(centre, nz - 1, 1)
                )
                free = lab[x + level, y + level] == 0
                target[x, y] = jnp.where(jnp.concatenate([free, free], 0), value, 0.0)
            return 0

        lax.fori_loop(0, rows, one_row, 0)
    for power in range(4):
        inset = DEPTH - 1 - power
        for x in range(nx):
            for y in range(ny):
                value = bufs[power + 1][x + inset, y + inset]
                cell = x * ny + y
                basis_ref[power * K : (power + 1) * K, cell * nz : (cell + 1) * nz] = value
                scaled[power * K : (power + 1) * K, cell * nz : (cell + 1) * nz] = value * diag
    gram = lax.dot_general(
        basis_ref[: 3 * K, :],
        scaled[...],
        (((1,), (1,)), ((), ())),
        precision=HIGHEST,
        preferred_element_type=jnp.float32,
    )
    gram = jnp.concatenate([gram, jnp.zeros((3 * K, 128 - 4 * K), jnp.float32)], 1)
    place = lax.broadcasted_iota(jnp.int32, (K, 128), 1)
    moments = jnp.where(
        place < 2 * K,
        gram[:K],
        jnp.where(
            place < 4 * K,
            pltpu.roll(gram[K : 2 * K], K, 1),
            jnp.where(place < 6 * K, pltpu.roll(gram[2 * K :], 2 * K, 1), 0.0),
        ),
    )
    for copy in range(moments_ref.shape[0]):
        moments_ref[copy] = moments


def outputs_kernel(parts_ref, basis_ref, index_ref, eps_ref, solution_ref, residual_ref):
    ny, nz = solution_ref.shape[2:]
    cells = solution_ref.shape[1] * ny
    _, _, _, diag, _ = plane_coefficients(index_ref, eps_ref)
    moments = parts_ref[0]
    for part in range(1, parts_ref.shape[0]):
        moments = moments + parts_ref[part]
    place = lax.broadcasted_iota(jnp.int32, (K, 128), 1)
    images = moments - pltpu.roll(moments, 128 - K, 1)
    blocks = []
    for power in range(3):
        left = images if power == 0 else pltpu.roll(images, 128 - power * K, 1)
        right = moments if power == 3 else pltpu.roll(moments, (3 - power) * K, 1)
        blocks.append(jnp.where(place < 3 * K, left, jnp.where(place < 4 * K, right, 0.0)))
    matrix = jnp.concatenate(blocks, 0)
    number = lax.broadcasted_iota(jnp.int32, (3 * K, 128), 0)
    for pivot in range(3 * K):
        line = matrix[pivot : pivot + 1, :]
        line = line * (1.0 / matrix[pivot : pivot + 1, pivot : pivot + 1])
        column = jnp.broadcast_to(matrix[:, pivot : pivot + 1], matrix.shape)
        matrix = jnp.where(number == pivot, line, matrix - column * line)
    weights = matrix[:, 3 * K : 4 * K].T
    first, second, third = weights[:, :K], weights[:, K : 2 * K], weights[:, 2 * K :]
    unit = (
        lax.broadcasted_iota(jnp.int32, (K, K), 0) == lax.broadcasted_iota(jnp.int32, (K, K), 1)
    ).astype(jnp.float32)
    combine = jnp.concatenate(
        [
            jnp.concatenate([first, second, third, jnp.zeros((K, K), jnp.float32)], 1),
            jnp.concatenate([unit - first, first - second, second - third, third], 1),
        ],
        0,
    )
    both = jnp.dot(combine, basis_ref[...], precision=HIGHEST, preferred_element_type=jnp.float32)
    for cell in range(cells):
        block = both[:, cell * nz : (cell + 1) * nz]
        solution_ref[:, cell // ny, cell % ny, :] = block[:K]
        residual_ref[:, cell // ny, cell % ny, :] = block[K:] * diag


def neighbours(block, axis):
    count = lax.axis_size(axis)
    forward = [(i, i + 1) for i in range(count - 1)]
    backward = [(target, source) for source, target in forward]
    return lax.ppermute(block, axis, forward), lax.ppermute(block, axis, backward)


def gathered(copies, axis):
    return lax.all_to_all(copies, axis, 0, 0, tiled=True)


def on_device(labels, layer_index, layer_eps):
    nx, ny, nz = labels.shape
    wide = ny + 2 * DEPTH
    in_x, in_y = lax.axis_size("gx"), lax.axis_size("gy")
    at_x, at_y = lax.axis_index("gx"), lax.axis_index("gy")
    before, after = neighbours(labels, "gy")
    mid = jnp.concatenate(
        [
            jnp.where(at_y > 0, before[:, ny - DEPTH :], -1),
            labels,
            jnp.where(at_y < in_y - 1, after[:, :DEPTH], -1),
        ],
        1,
    )
    low, high = neighbours(mid, "gx")
    place = jnp.stack([at_x > 0, at_x >= 0, at_x < in_x - 1]).astype(jnp.int32)
    index = layer_index.reshape(1, nz)
    vmem, smem = pl.BlockSpec(memory_space=pltpu.VMEM), pl.BlockSpec(memory_space=pltpu.SMEM)
    rows = 3 * nx
    basis, moments = pl.pallas_call(
        basis_kernel,
        out_shape=(
            jax.ShapeDtypeStruct((4 * K, nx * ny * nz), jnp.float32),
            jax.ShapeDtypeStruct((in_y, K, 128), jnp.float32),
        ),
        in_specs=[smem, vmem, vmem, vmem, vmem, smem],
        out_specs=(vmem, vmem),
        scratch_shapes=[pltpu.VMEM((rows, wide, 8, nz), jnp.int32)]
        + [pltpu.VMEM((rows - 2 * i, wide - 2 * i, K, nz), jnp.float32) for i in range(4)]
        + [pltpu.VMEM((4 * K, nx * ny * nz), jnp.float32)],
        compiler_params=pltpu.CompilerParams(vmem_limit_bytes=16 << 20),
    )(place, mid, low, high, index, layer_eps)
    total = gathered(moments, "gy").sum(0)
    parts = gathered(jnp.broadcast_to(total[None], (in_x,) + total.shape), "gx")
    block = jax.ShapeDtypeStruct((K, nx, ny, nz), jnp.float32)
    return pl.pallas_call(
        outputs_kernel,
        out_shape=(block, block),
        in_specs=[vmem, vmem, vmem, smem],
        out_specs=(vmem, vmem),
        compiler_params=pltpu.CompilerParams(vmem_limit_bytes=16 << 20),
    )(parts, basis, index, layer_eps)


def solution(mesh):
    return jax.shard_map(
        on_device,
        mesh=mesh,
        in_specs=(P("gx", "gy", None), P(), P()),
        out_specs=(P(None, "gx", "gy", None), P(None, "gx", "gy", None)),
        check_vma=False,
    )
```

```python
import jax
import jax.numpy as jnp
from jax import lax
from jax.experimental import pallas as pl
from jax.experimental.pallas import tpu as pltpu
from jax.sharding import PartitionSpec as P

K = 16
STEPS = 3
DEPTH = STEPS + 1
ROWS = 8
LANES = 128
F32, BF16 = jnp.float32, jnp.bfloat16


def split(value):
    high = value.astype(BF16)
    rest = value - high.astype(F32)
    middle = rest.astype(BF16)
    return high, middle, (rest - middle.astype(F32)).astype(BF16)


def basis_kernel(low_ref, mid_ref, high_ref, coef_ref, split_ref, moments_ref, weight, b0, b1, b2, b3):
    nx, wide, nz = mid_ref.shape
    ny = wide - 2 * DEPTH

    def beyond(x, y):
        return max(nx - x, 0, x - 2 * nx + 1) + max(DEPTH - y, 0, y - DEPTH - ny + 1)

    shape = (K, nz)
    lateral_c, below_c, above_c, root = (jnp.broadcast_to(coef_ref[i : i + 1, :], shape) for i in range(4))
    number = lax.broadcasted_iota(jnp.int32, shape, 0) + 1
    for x in range(3 * nx):
        ref = (low_ref, mid_ref, high_ref)[x // nx]
        for y in range(wide):
            if beyond(x, y) <= DEPTH:
                label = jnp.broadcast_to(ref[x % nx, y : y + 1, :], shape)
                b0[x, y] = (label == number).astype(F32)
                if beyond(x, y) < DEPTH:
                    weight[x, y] = jnp.where(label == 0, lateral_c, 0.0)[:ROWS]
    powers = (b0, b1, b2, b3)
    for level in range(1, DEPTH + 1):
        source = powers[level - 1]
        for x in range(3 * nx):
            for y in range(wide):
                if beyond(x, y) > DEPTH - level:
                    continue
                centre = source[x, y]
                lateral = (source[x - 1, y] + source[x + 1, y]) + (source[x, y - 1] + source[x, y + 1])
                vertical = below_c * pltpu.roll(centre, 1, 1) + above_c * pltpu.roll(centre, nz - 1, 1)
                factor = weight[x, y]
                value = jnp.concatenate([factor, factor], 0) * (lateral + vertical)
                if level < DEPTH:
                    powers[level][x, y] = value
                if beyond(x, y) == 0:
                    cell = (x - nx) * ny + y - DEPTH
                    for part, piece in enumerate(split(value * root)):
                        first = (part * DEPTH + level - 1) * K
                        split_ref[first : first + K, cell * nz : (cell + 1) * nz] = piece
    size, used = DEPTH * K, STEPS * K
    grams = lax.dot_general(
        jnp.concatenate([split_ref[part * size : part * size + used, :] for part in range(3)], 0),
        split_ref[...],
        (((1,), (1,)), ((), ())),
        preferred_element_type=F32,
    )

    def piece(i, j):
        return grams[i * used : (i + 1) * used, j * size : (j + 1) * size]

    gram = piece(0, 0) + ((piece(0, 1) + piece(1, 0)) + ((piece(0, 2) + piece(2, 0)) + piece(1, 1)))
    gram = jnp.concatenate([gram, jnp.zeros((used, LANES - size), F32)], 1)
    lane = lax.broadcasted_iota(jnp.int32, (K, LANES), 1)
    row = lax.broadcasted_iota(jnp.int32, (K, LANES), 0)
    packed = jnp.zeros((K, LANES), F32)
    for pair in range(3):
        start = pair * (K + 1)
        left, right = (pair + 3) // 2, pair // 2
        lower = pltpu.roll(gram[left * K : (left + 1) * K], (start - (pair + 4) // 2 * K) % LANES, 1)
        upper = pltpu.roll(gram[right * K : (right + 1) * K], (start + 1 - (pair + 1) // 2 * K) % LANES, 1)
        inside = (lane >= start) & (lane < start + K + 1)
        packed = jnp.where(inside, jnp.where(lane - start <= row, lower, upper), packed)
    folded = packed[:ROWS] + pltpu.roll(packed[ROWS:], LANES // 2, 1)
    for copy in range(moments_ref.shape[0]):
        moments_ref[copy] = folded


def eliminate(matrix):
    tiles = len(matrix)
    sub = lax.broadcasted_iota(jnp.int32, (ROWS, LANES), 0)
    for block in range(tiles):
        columns = [
            [
                jnp.broadcast_to(tile[:, block * ROWS + j : block * ROWS + j + 1], (ROWS, LANES))
                for tile in matrix
            ]
            for j in range(ROWS)
        ]
        for j in range(ROWS):
            column = columns[j]
            inverse = 1.0 / column[block][j : j + 1]
            line = matrix[block][j : j + 1] * inverse
            for later in range(j + 1, ROWS):
                other = columns[later]
                share = other[block][j : j + 1] * inverse
                columns[later] = [
                    jnp.where(sub == j, share, other[t] - column[t] * share) if t == block else other[t] - column[t] * share
                    for t in range(tiles)
                ]
            matrix = [
                jnp.where(sub == j, line, matrix[t] - column[t] * line) if t == block else matrix[t] - column[t] * line
                for t in range(tiles)
            ]
    return matrix


def outputs_kernel(parts_ref, split_ref, coef_ref, solution_ref, residual_ref, turned):
    ny, nz = solution_ref.shape[2:]
    cells = solution_ref.shape[1] * ny
    sums = [parts_ref[part] for part in range(parts_ref.shape[0])]
    while len(sums) > 1:
        sums = [a + b for a, b in zip(sums[::2], sums[1::2])]
    folded = sums[0]
    packed = jnp.concatenate([folded, pltpu.roll(folded, LANES // 2, 1)], 0)
    turned[...] = packed.T
    lane = lax.broadcasted_iota(jnp.int32, (K, LANES), 1)
    row = lax.broadcasted_iota(jnp.int32, (K, LANES), 0)
    moments = jnp.zeros((K, LANES), F32)
    for power in range(2 * STEPS):
        pair, upper = power % 3, power < 3
        start = pair * (K + 1) + upper
        mirrored = jnp.concatenate([turned[start : start + K, :], jnp.zeros((K, LANES - K), F32)], 1)
        direct = pltpu.roll(packed, (power * K - start) % LANES, 1)
        mirrored = pltpu.roll(mirrored, power * K, 1) if power else mirrored
        column = lane - power * K
        chosen = jnp.where(column >= row, direct, mirrored) if upper else jnp.where(column <= row, direct, mirrored)
        moments = jnp.where((column >= 0) & (column < K), chosen, moments)
    images = moments - pltpu.roll(moments, LANES - K, 1)
    matrix = []
    for power in range(STEPS):
        left = images if power == 0 else pltpu.roll(images, LANES - power * K, 1)
        right = pltpu.roll(moments, (STEPS - power) * K, 1)
        block = jnp.where(lane < STEPS * K, left, right)
        matrix += [block[:ROWS], block[ROWS:]]
    matrix = jnp.concatenate(eliminate(matrix), 0)
    weights = matrix[:, STEPS * K : (STEPS + 1) * K].T
    first, second, third = weights[:, :K], weights[:, K : 2 * K], weights[:, 2 * K :]
    unit = (
        lax.broadcasted_iota(jnp.int32, (K, K), 0) == lax.broadcasted_iota(jnp.int32, (K, K), 1)
    ).astype(F32)
    none = jnp.zeros((K, K), F32)
    combine = jnp.concatenate(
        [
            jnp.concatenate([first, second, third, none], 1),
            jnp.concatenate([unit - first, first - second, second - third, third], 1),
        ],
        0,
    )
    high, middle, low = split(combine)
    zero = jnp.zeros(high.shape, BF16)
    factors = jnp.concatenate(
        [
            jnp.concatenate([high, high, high], 1),
            jnp.concatenate([middle, middle, zero], 1),
            jnp.concatenate([low, zero, zero], 1),
        ],
        0,
    )
    both = jnp.dot(factors, split_ref[...], preferred_element_type=F32)
    count = 2 * K
    both = both[:count] + (both[count : 2 * count] + both[2 * count :])
    root, over = coef_ref[3:4, :], coef_ref[4:5, :]
    for cell in range(cells):
        block = both[:, cell * nz : (cell + 1) * nz]
        solution_ref[:, cell // ny, cell % ny, :] = block[:K] * over
        residual_ref[:, cell // ny, cell % ny, :] = block[K:] * root


def coefficients(layer_index, layer_eps):
    layers = jnp.arange(layer_eps.shape[0], dtype=jnp.int32)
    eps = jnp.where(layer_index[None, :] == layers[:, None], layer_eps[:, None], 0.0).sum(0)
    middle = 0.5 * (eps[1:] + eps[:-1])
    nothing = jnp.zeros((1,), F32)
    down = jnp.concatenate([eps[:1], middle])
    up = jnp.concatenate([middle, eps[-1:]])
    diag = 4.0 * eps + down + up
    below = jnp.concatenate([nothing, middle]) / eps
    above = jnp.concatenate([middle, nothing]) / eps
    root = jnp.sqrt(diag)
    blank = jnp.zeros_like(eps)
    return jnp.stack([eps / diag, below, above, root, 1.0 / root, blank, blank, blank])


def neighbours(block, axis):
    count, at = lax.axis_size(axis), lax.axis_index(axis)
    even = lax.ppermute(block, axis, [(i, i ^ 1) for i in range(count)])
    pairs = [(i, i + 1) for i in range(1, count - 1, 2)]
    odd = lax.ppermute(block, axis, pairs + [(j, i) for i, j in pairs])
    second = at % 2 == 1
    before = jnp.where(second, even, jnp.where(at > 0, odd, -1))
    after = jnp.where(second, jnp.where(at < count - 1, odd, -1), even)
    return before, after


def gathered(copies, axis):
    return lax.all_to_all(copies, axis, 0, 0, tiled=True)


def on_device(labels, layer_index, layer_eps):
    nx, ny, nz = labels.shape
    wide, rows = ny + 2 * DEPTH, 3 * nx
    before, after = neighbours(labels, "gy")
    mid = jnp.concatenate([before[:, ny - DEPTH :], labels, after[:, :DEPTH]], 1)
    low, high = neighbours(mid, "gx")
    coef = coefficients(layer_index, layer_eps)
    vmem = pl.BlockSpec(memory_space=pltpu.VMEM)
    params = pltpu.CompilerParams(vmem_limit_bytes=16 << 20)
    in_x, in_y = lax.axis_size("gx"), lax.axis_size("gy")
    field = pltpu.VMEM((rows, wide, K, nz), F32)
    parts, moments = pl.pallas_call(
        basis_kernel,
        out_shape=(
            jax.ShapeDtypeStruct((3 * DEPTH * K, nx * ny * nz), BF16),
            jax.ShapeDtypeStruct((in_y, ROWS, LANES), F32),
        ),
        in_specs=[vmem] * 4,
        out_specs=(vmem, vmem),
        scratch_shapes=[pltpu.VMEM((rows, wide, ROWS, nz), F32), field, field, field, field],
        compiler_params=params,
    )(low, mid, high, coef)
    total = gathered(moments, "gy").sum(0)
    sums = gathered(jnp.broadcast_to(total[None], (in_x,) + total.shape), "gx")
    block = jax.ShapeDtypeStruct((K, nx, ny, nz), F32)
    return pl.pallas_call(
        outputs_kernel,
        out_shape=(block, block),
        in_specs=[vmem] * 3,
        out_specs=(vmem, vmem),
        scratch_shapes=[pltpu.VMEM((LANES, K), F32)],
        compiler_params=params,
    )(sums, parts, coef)


def solution(mesh):
    return jax.shard_map(
        on_device,
        mesh=mesh,
        in_specs=(P("gx", "gy", None), P(), P()),
        out_specs=(P(None, "gx", "gy", None), P(None, "gx", "gy", None)),
        check_vma=False,
    )
```

```python
import jax
import jax.numpy as jnp
from jax import lax
from jax.experimental import pallas as pl
from jax.experimental.pallas import tpu as pltpu
from jax.sharding import PartitionSpec as P

K = 16
STEPS = 3
DEPTH = STEPS + 1
ROWS = 8
LANES = 128
F32, BF16 = jnp.float32, jnp.bfloat16


def split(value):
    high = value.astype(BF16)
    rest = value - high.astype(F32)
    middle = rest.astype(BF16)
    return high, middle, (rest - middle.astype(F32)).astype(BF16)


def basis_kernel(low_ref, mid_ref, high_ref, coef_ref, split_ref, moments_ref, weight, b0, b1, b2, b3):
    nx, wide, nz = mid_ref.shape
    ny = wide - 2 * DEPTH

    def beyond(x, y):
        return max(nx - x, 0, x - 2 * nx + 1) + max(DEPTH - y, 0, y - DEPTH - ny + 1)

    shape = (K, nz)
    lateral_c, below_c, above_c, root = (jnp.broadcast_to(coef_ref[i : i + 1, :], shape) for i in range(4))
    number = lax.broadcasted_iota(jnp.int32, shape, 0) + 1
    for x in range(3 * nx):
        ref = (low_ref, mid_ref, high_ref)[x // nx]
        for y in range(wide):
            if beyond(x, y) <= DEPTH:
                label = jnp.broadcast_to(ref[x % nx, y : y + 1, :], shape)
                b0[x, y] = (label == number).astype(F32)
                if beyond(x, y) < DEPTH:
                    weight[x, y] = jnp.where(label == 0, lateral_c, 0.0)[:ROWS]
    powers = (b0, b1, b2, b3)
    for level in range(1, DEPTH + 1):
        source = powers[level - 1]
        for x in range(3 * nx):
            for y in range(wide):
                if beyond(x, y) > DEPTH - level:
                    continue
                centre = source[x, y]
                lateral = (source[x - 1, y] + source[x + 1, y]) + (source[x, y - 1] + source[x, y + 1])
                vertical = below_c * pltpu.roll(centre, 1, 1) + above_c * pltpu.roll(centre, nz - 1, 1)
                factor = weight[x, y]
                value = jnp.concatenate([factor, factor], 0) * (lateral + vertical)
                if level < DEPTH:
                    powers[level][x, y] = value
                if beyond(x, y) == 0:
                    cell = (x - nx) * ny + y - DEPTH
                    for part, piece in enumerate(split(value * root)):
                        first = (part * DEPTH + level - 1) * K
                        split_ref[first : first + K, cell * nz : (cell + 1) * nz] = piece
    size, used = DEPTH * K, STEPS * K
    grams = lax.dot_general(
        jnp.concatenate([split_ref[part * size : part * size + used, :] for part in range(3)], 0),
        split_ref[...],
        (((1,), (1,)), ((), ())),
        preferred_element_type=F32,
    )

    def piece(i, j):
        return grams[i * used : (i + 1) * used, j * size : (j + 1) * size]

    gram = piece(0, 0) + ((piece(0, 1) + piece(1, 0)) + ((piece(0, 2) + piece(2, 0)) + piece(1, 1)))
    gram = jnp.concatenate([gram, jnp.zeros((used, LANES - size), F32)], 1)
    lane = lax.broadcasted_iota(jnp.int32, (K, LANES), 1)
    row = lax.broadcasted_iota(jnp.int32, (K, LANES), 0)
    packed = jnp.zeros((K, LANES), F32)
    for pair in range(3):
        start = pair * (K + 1)
        left, right = (pair + 3) // 2, pair // 2
        lower = pltpu.roll(gram[left * K : (left + 1) * K], (start - (pair + 4) // 2 * K) % LANES, 1)
        upper = pltpu.roll(gram[right * K : (right + 1) * K], (start + 1 - (pair + 1) // 2 * K) % LANES, 1)
        inside = (lane >= start) & (lane < start + K + 1)
        packed = jnp.where(inside, jnp.where(lane - start <= row, lower, upper), packed)
    folded = packed[:ROWS] + pltpu.roll(packed[ROWS:], LANES // 2, 1)
    for copy in range(moments_ref.shape[0]):
        moments_ref[copy] = folded


def eliminate(matrix):
    tiles = len(matrix)
    sub = lax.broadcasted_iota(jnp.int32, (ROWS, LANES), 0)
    for block in range(tiles):
        columns = [
            [
                jnp.broadcast_to(tile[:, block * ROWS + j : block * ROWS + j + 1], (ROWS, LANES))
                for tile in matrix
            ]
            for j in range(ROWS)
        ]
        for j in range(ROWS):
            column = columns[j]
            inverse = 1.0 / column[block][j : j + 1]
            line = matrix[block][j : j + 1] * inverse
            for later in range(j + 1, ROWS):
                other = columns[later]
                share = other[block][j : j + 1] * inverse
                columns[later] = [
                    jnp.where(sub == j, share, other[t] - column[t] * share) if t == block else other[t] - column[t] * share
                    for t in range(tiles)
                ]
            matrix = [
                jnp.where(sub == j, line, matrix[t] - column[t] * line) if t == block else matrix[t] - column[t] * line
                for t in range(tiles)
            ]
    return matrix


def outputs_kernel(parts_ref, split_ref, coef_ref, solution_ref, residual_ref, turned):
    ny, nz = solution_ref.shape[2:]
    cells = solution_ref.shape[1] * ny
    sums = [parts_ref[part] for part in range(parts_ref.shape[0])]
    while len(sums) > 1:
        sums = [a + b for a, b in zip(sums[::2], sums[1::2])]
    folded = sums[0]
    packed = jnp.concatenate([folded, pltpu.roll(folded, LANES // 2, 1)], 0)
    turned[...] = packed.T
    lane = lax.broadcasted_iota(jnp.int32, (K, LANES), 1)
    row = lax.broadcasted_iota(jnp.int32, (K, LANES), 0)
    moments = jnp.zeros((K, LANES), F32)
    for power in range(2 * STEPS):
        pair, upper = power % 3, power < 3
        start = pair * (K + 1) + upper
        mirrored = jnp.concatenate([turned[start : start + K, :], jnp.zeros((K, LANES - K), F32)], 1)
        direct = pltpu.roll(packed, (power * K - start) % LANES, 1)
        mirrored = pltpu.roll(mirrored, power * K, 1) if power else mirrored
        column = lane - power * K
        chosen = jnp.where(column >= row, direct, mirrored) if upper else jnp.where(column <= row, direct, mirrored)
        moments = jnp.where((column >= 0) & (column < K), chosen, moments)
    images = moments - pltpu.roll(moments, LANES - K, 1)
    matrix = []
    for power in range(STEPS):
        left = images if power == 0 else pltpu.roll(images, LANES - power * K, 1)
        right = pltpu.roll(moments, (STEPS - power) * K, 1)
        block = jnp.where(lane < STEPS * K, left, right)
        matrix += [block[:ROWS], block[ROWS:]]
    matrix = jnp.concatenate(eliminate(matrix), 0)
    weights = matrix[:, STEPS * K : (STEPS + 1) * K].T
    first, second, third = weights[:, :K], weights[:, K : 2 * K], weights[:, 2 * K :]
    unit = (
        lax.broadcasted_iota(jnp.int32, (K, K), 0) == lax.broadcasted_iota(jnp.int32, (K, K), 1)
    ).astype(F32)
    none = jnp.zeros((K, K), F32)
    combine = jnp.concatenate(
        [
            jnp.concatenate([first, second, third, none], 1),
            jnp.concatenate([unit - first, first - second, second - third, third], 1),
        ],
        0,
    )
    high, middle, low = split(combine)
    zero = jnp.zeros(high.shape, BF16)
    factors = jnp.concatenate(
        [
            jnp.concatenate([high, high, high], 1),
            jnp.concatenate([middle, middle, zero], 1),
            jnp.concatenate([low, zero, zero], 1),
        ],
        0,
    )
    both = jnp.dot(factors, split_ref[...], preferred_element_type=F32)
    count = 2 * K
    both = both[:count] + (both[count : 2 * count] + both[2 * count :])
    root, over = coef_ref[3:4, :], coef_ref[4:5, :]
    for cell in range(cells):
        block = both[:, cell * nz : (cell + 1) * nz]
        solution_ref[:, cell // ny, cell % ny, :] = block[:K] * over
        residual_ref[:, cell // ny, cell % ny, :] = block[K:] * root


def plane_kernel(index_ref, eps_ref, late_ref, coef_ref):
    del late_ref
    index = index_ref[...]
    eps = jnp.zeros(index.shape, F32)
    for layer in range(eps_ref.shape[1]):
        eps = jnp.where(index == layer, jnp.broadcast_to(eps_ref[:, layer : layer + 1], index.shape), eps)
    count = index.shape[1]
    lane = lax.broadcasted_iota(jnp.int32, index.shape, 1)
    down = jnp.where(lane == 0, eps, 0.5 * (eps + pltpu.roll(eps, 1, 1)))
    up = jnp.where(lane == count - 1, eps, 0.5 * (eps + pltpu.roll(eps, count - 1, 1)))
    diag = 4.0 * eps + down + up
    root = jnp.sqrt(diag)
    coef_ref[0:1, :] = eps / diag
    coef_ref[1:2, :] = jnp.where(lane == 0, 0.0, down / eps)
    coef_ref[2:3, :] = jnp.where(lane == count - 1, 0.0, up / eps)
    coef_ref[3:4, :] = root
    coef_ref[4:5, :] = 1.0 / root


def hold_kernel(given_ref, held_ref):
    held_ref[...] = given_ref[...]


def neighbours(block, axis):
    count, at = lax.axis_size(axis), lax.axis_index(axis)
    even = lax.ppermute(block, axis, [(i, i ^ 1) for i in range(count)])
    pairs = [(i, i + 1) for i in range(1, count - 1, 2)]
    odd = lax.ppermute(block, axis, pairs + [(j, i) for i, j in pairs])
    first = at % 2 == 0
    if axis == "gy":
        before = jnp.where(first, jnp.where(at > 0, odd, -1), even)
        after = jnp.where(first, even, jnp.where(at < count - 1, odd, -1))
    else:
        before = jnp.where(~first, even, jnp.where(at > 0, odd, -1))
        after = jnp.where(~first, jnp.where(at < count - 1, odd, -1), even)
    return before, after


def gathered(copies, axis):
    return lax.all_to_all(copies, axis, 0, 0, tiled=True)


def on_device(labels, layer_index, layer_eps):
    nx, ny, nz = labels.shape
    wide, rows = ny + 2 * DEPTH, 3 * nx
    vmem = pl.BlockSpec(memory_space=pltpu.VMEM)
    params = pltpu.CompilerParams(vmem_limit_bytes=16 << 20)
    held = pl.pallas_call(
        hold_kernel,
        out_shape=jax.ShapeDtypeStruct(labels.shape, labels.dtype),
        in_specs=[vmem],
        out_specs=vmem,
        compiler_params=params,
    )(labels)
    before, after = neighbours(labels, "gy")
    mid = jnp.concatenate([before[:, ny - DEPTH :], held, after[:, :DEPTH]], 1)
    low, high = neighbours(mid, "gx")
    coef = pl.pallas_call(
        plane_kernel,
        out_shape=jax.ShapeDtypeStruct((ROWS, nz), F32),
        in_specs=[vmem, vmem, pl.BlockSpec(memory_space=pl.ANY)],
        out_specs=vmem,
        compiler_params=params,
    )(layer_index.reshape(1, nz), layer_eps.reshape(1, -1), mid)
    in_x, in_y = lax.axis_size("gx"), lax.axis_size("gy")
    field = pltpu.VMEM((rows, wide, K, nz), F32)
    parts, moments = pl.pallas_call(
        basis_kernel,
        out_shape=(
            jax.ShapeDtypeStruct((3 * DEPTH * K, nx * ny * nz), BF16),
            jax.ShapeDtypeStruct((in_y, ROWS, LANES), F32),
        ),
        in_specs=[vmem] * 4,
        out_specs=(vmem, vmem),
        scratch_shapes=[pltpu.VMEM((rows, wide, ROWS, nz), F32), field, field, field, field],
        compiler_params=params,
    )(low, mid, high, coef)
    total = gathered(moments, "gy").sum(0)
    sums = gathered(jnp.broadcast_to(total[None], (in_x,) + total.shape), "gx")
    block = jax.ShapeDtypeStruct((K, nx, ny, nz), F32)
    return pl.pallas_call(
        outputs_kernel,
        out_shape=(block, block),
        in_specs=[vmem] * 3,
        out_specs=(vmem, vmem),
        scratch_shapes=[pltpu.VMEM((LANES, K), F32)],
        compiler_params=params,
    )(sums, parts, coef)


def solution(mesh):
    return jax.shard_map(
        on_device,
        mesh=mesh,
        in_specs=(P("gx", "gy", None), P(), P()),
        out_specs=(P(None, "gx", "gy", None), P(None, "gx", "gy", None)),
        check_vma=False,
    )
```

```python
import jax
import jax.numpy as jnp
from jax import lax
from jax.experimental import pallas as pl
from jax.experimental.pallas import tpu as pltpu
from jax.sharding import PartitionSpec as P

K = 16
STEPS = 3
DEPTH = STEPS + 1
ROWS = 8
LANES = 128
F32, BF16 = jnp.float32, jnp.bfloat16


def split(value):
    high = value.astype(BF16)
    rest = value - high.astype(F32)
    middle = rest.astype(BF16)
    return high, middle, (rest - middle.astype(F32)).astype(BF16)


def beyond(x, y, nx, ny):
    return max(nx - x, 0, x - 2 * nx + 1) + max(DEPTH - y, 0, y - DEPTH - ny + 1)


def is_early(level, x, y, nx, ny):
    return DEPTH + level <= y < DEPTH + ny - level and level <= x < 3 * nx - level


def excite(label, lateral_c):
    label = jnp.broadcast_to(label, lateral_c.shape)
    number = lax.broadcasted_iota(jnp.int32, lateral_c.shape, 0) + 1
    return (label == number).astype(F32), jnp.where(label == 0, lateral_c, 0.0)[:ROWS]


def next_power(x, y, power, factor, below_c, above_c):
    centre = power(x, y)
    lateral = (power(x - 1, y) + power(x + 1, y)) + (power(x, y - 1) + power(x, y + 1))
    last = centre.shape[1] - 1
    vertical = below_c * pltpu.roll(centre, 1, 1) + above_c * pltpu.roll(centre, last, 1)
    return jnp.concatenate([factor, factor], 0) * (lateral + vertical)


def early_kernel(centre_ref, coef_ref, weight, b0, b1, b2, b3):
    rows, ny, nz = centre_ref.shape
    nx = rows // 3
    lateral_c, below_c, above_c = (jnp.broadcast_to(coef_ref[i : i + 1, :], (K, nz)) for i in range(3))
    for x in range(rows):
        for y in range(ny):
            b0[x, y], weight[x, y] = excite(centre_ref[x, y : y + 1, :], lateral_c)
    powers = (b0, b1, b2, b3)
    for level in range(1, DEPTH):
        source = powers[level - 1]
        for x in range(rows):
            for y in range(ny):
                if is_early(level, x, y + DEPTH, nx, ny):
                    powers[level][x, y] = next_power(
                        x, y, lambda i, j, source=source: source[i, j], weight[x, y], below_c, above_c
                    )


def basis_kernel(left_ref, right_ref, coef_ref, early_weight, e0, e1, e2, e3, split_ref, moments_ref, weight, b0, b1, b2, b3):
    rows, ny, _, nz = early_weight.shape
    nx, wide = rows // 3, ny + 2 * DEPTH
    lateral_c, below_c, above_c, root = (jnp.broadcast_to(coef_ref[i : i + 1, :], (K, nz)) for i in range(4))
    for x in range(rows):
        for y in range(wide):
            if beyond(x, y, nx, ny) <= DEPTH and not is_early(0, x, y, nx, ny):
                ref, at = (left_ref, y) if y < DEPTH else (right_ref, y - DEPTH - ny)
                b0[x, y], weight[x, y] = excite(ref[x, at : at + 1, :], lateral_c)
    early, late = (e0, e1, e2, e3), (b0, b1, b2, b3)

    def power(level, x, y):
        return early[level][x, y - DEPTH] if is_early(level, x, y, nx, ny) else late[level][x, y]

    for level in range(1, DEPTH + 1):
        for x in range(rows):
            for y in range(wide):
                if beyond(x, y, nx, ny) > DEPTH - level:
                    continue
                if is_early(level, x, y, nx, ny):
                    value = power(level, x, y)
                else:
                    factor = early_weight[x, y - DEPTH] if is_early(0, x, y, nx, ny) else weight[x, y]
                    value = next_power(
                        x, y, lambda i, j, level=level: power(level - 1, i, j), factor, below_c, above_c
                    )
                    if level < DEPTH:
                        late[level][x, y] = value
                if beyond(x, y, nx, ny) == 0:
                    cell = (x - nx) * ny + y - DEPTH
                    for part, piece in enumerate(split(value * root)):
                        first = (part * DEPTH + level - 1) * K
                        split_ref[first : first + K, cell * nz : (cell + 1) * nz] = piece
    size, used = DEPTH * K, STEPS * K
    grams = lax.dot_general(
        jnp.concatenate([split_ref[part * size : part * size + used, :] for part in range(3)], 0),
        split_ref[...],
        (((1,), (1,)), ((), ())),
        preferred_element_type=F32,
    )

    def piece(i, j):
        return grams[i * used : (i + 1) * used, j * size : (j + 1) * size]

    gram = piece(0, 0) + ((piece(0, 1) + piece(1, 0)) + ((piece(0, 2) + piece(2, 0)) + piece(1, 1)))
    gram = jnp.concatenate([gram, jnp.zeros((used, LANES - size), F32)], 1)
    lane = lax.broadcasted_iota(jnp.int32, (K, LANES), 1)
    row = lax.broadcasted_iota(jnp.int32, (K, LANES), 0)
    packed = jnp.zeros((K, LANES), F32)
    for pair in range(3):
        start = pair * (K + 1)
        left, right = (pair + 3) // 2, pair // 2
        lower = pltpu.roll(gram[left * K : (left + 1) * K], (start - (pair + 4) // 2 * K) % LANES, 1)
        upper = pltpu.roll(gram[right * K : (right + 1) * K], (start + 1 - (pair + 1) // 2 * K) % LANES, 1)
        inside = (lane >= start) & (lane < start + K + 1)
        packed = jnp.where(inside, jnp.where(lane - start <= row, lower, upper), packed)
    folded = packed[:ROWS] + pltpu.roll(packed[ROWS:], LANES // 2, 1)
    for copy in range(moments_ref.shape[0]):
        moments_ref[copy] = folded


def eliminate(matrix):
    tiles = len(matrix)
    sub = lax.broadcasted_iota(jnp.int32, (ROWS, LANES), 0)
    for block in range(tiles):
        columns = [
            [
                jnp.broadcast_to(tile[:, block * ROWS + j : block * ROWS + j + 1], (ROWS, LANES))
                for tile in matrix
            ]
            for j in range(ROWS)
        ]
        for j in range(ROWS):
            column = columns[j]
            inverse = 1.0 / column[block][j : j + 1]
            line = matrix[block][j : j + 1] * inverse
            for later in range(j + 1, ROWS):
                other = columns[later]
                share = other[block][j : j + 1] * inverse
                columns[later] = [
                    jnp.where(sub == j, share, other[t] - column[t] * share) if t == block else other[t] - column[t] * share
                    for t in range(tiles)
                ]
            matrix = [
                jnp.where(sub == j, line, matrix[t] - column[t] * line) if t == block else matrix[t] - column[t] * line
                for t in range(tiles)
            ]
    return matrix


def outputs_kernel(parts_ref, split_ref, coef_ref, solution_ref, residual_ref, turned):
    ny, nz = solution_ref.shape[2:]
    cells = solution_ref.shape[1] * ny
    sums = [parts_ref[part] for part in range(parts_ref.shape[0])]
    while len(sums) > 1:
        sums = [a + b for a, b in zip(sums[::2], sums[1::2])]
    folded = sums[0]
    packed = jnp.concatenate([folded, pltpu.roll(folded, LANES // 2, 1)], 0)
    turned[...] = packed.T
    lane = lax.broadcasted_iota(jnp.int32, (K, LANES), 1)
    row = lax.broadcasted_iota(jnp.int32, (K, LANES), 0)
    moments = jnp.zeros((K, LANES), F32)
    for power in range(2 * STEPS):
        pair, upper = power % 3, power < 3
        start = pair * (K + 1) + upper
        mirrored = jnp.concatenate([turned[start : start + K, :], jnp.zeros((K, LANES - K), F32)], 1)
        direct = pltpu.roll(packed, (power * K - start) % LANES, 1)
        mirrored = pltpu.roll(mirrored, power * K, 1) if power else mirrored
        column = lane - power * K
        chosen = jnp.where(column >= row, direct, mirrored) if upper else jnp.where(column <= row, direct, mirrored)
        moments = jnp.where((column >= 0) & (column < K), chosen, moments)
    images = moments - pltpu.roll(moments, LANES - K, 1)
    matrix = []
    for power in range(STEPS):
        left = images if power == 0 else pltpu.roll(images, LANES - power * K, 1)
        right = pltpu.roll(moments, (STEPS - power) * K, 1)
        block = jnp.where(lane < STEPS * K, left, right)
        matrix += [block[:ROWS], block[ROWS:]]
    matrix = jnp.concatenate(eliminate(matrix), 0)
    weights = matrix[:, STEPS * K : (STEPS + 1) * K].T
    first, second, third = weights[:, :K], weights[:, K : 2 * K], weights[:, 2 * K :]
    unit = (
        lax.broadcasted_iota(jnp.int32, (K, K), 0) == lax.broadcasted_iota(jnp.int32, (K, K), 1)
    ).astype(F32)
    none = jnp.zeros((K, K), F32)
    combine = jnp.concatenate(
        [
            jnp.concatenate([first, second, third, none], 1),
            jnp.concatenate([unit - first, first - second, second - third, third], 1),
        ],
        0,
    )
    high, middle, low = split(combine)
    zero = jnp.zeros(high.shape, BF16)
    factors = jnp.concatenate(
        [
            jnp.concatenate([high, high, high], 1),
            jnp.concatenate([middle, middle, zero], 1),
            jnp.concatenate([low, zero, zero], 1),
        ],
        0,
    )
    both = jnp.dot(factors, split_ref[...], preferred_element_type=F32)
    count = 2 * K
    both = both[:count] + (both[count : 2 * count] + both[2 * count :])
    root, over = coef_ref[3:4, :], coef_ref[4:5, :]
    for cell in range(cells):
        block = both[:, cell * nz : (cell + 1) * nz]
        solution_ref[:, cell // ny, cell % ny, :] = block[:K] * over
        residual_ref[:, cell // ny, cell % ny, :] = block[K:] * root


def plane_kernel(labels_ref, index_ref, eps_ref, held_ref, coef_ref):
    held_ref[...] = labels_ref[...]
    index = index_ref[...]
    eps = jnp.zeros(index.shape, F32)
    for layer in range(eps_ref.shape[1]):
        eps = jnp.where(index == layer, jnp.broadcast_to(eps_ref[:, layer : layer + 1], index.shape), eps)
    count = index.shape[1]
    lane = lax.broadcasted_iota(jnp.int32, index.shape, 1)
    down = jnp.where(lane == 0, eps, 0.5 * (eps + pltpu.roll(eps, 1, 1)))
    up = jnp.where(lane == count - 1, eps, 0.5 * (eps + pltpu.roll(eps, count - 1, 1)))
    diag = 4.0 * eps + down + up
    root = jnp.sqrt(diag)
    coef_ref[0:1, :] = eps / diag
    coef_ref[1:2, :] = jnp.where(lane == 0, 0.0, down / eps)
    coef_ref[2:3, :] = jnp.where(lane == count - 1, 0.0, up / eps)
    coef_ref[3:4, :] = root
    coef_ref[4:5, :] = 1.0 / root


def neighbours(to_even, to_odd, axis):
    count, at = lax.axis_size(axis), lax.axis_index(axis)
    pairs = [(i, i + 1) for i in range(1, count - 1, 2)]
    odd = lax.ppermute(to_odd, axis, pairs + [(j, i) for i, j in pairs])
    even = lax.ppermute(to_even, axis, [(i, i ^ 1) for i in range(count)])
    first = at % 2 == 0
    before = jnp.where(first, jnp.where(at > 0, odd, -1), even)
    after = jnp.where(first, even, jnp.where(at < count - 1, odd, -1))
    return before, after


def gathered(copies, axis):
    return lax.all_to_all(copies, axis, 0, 0, tiled=True)


def on_device(labels, layer_index, layer_eps):
    nx, ny, nz = labels.shape
    wide, rows = ny + 2 * DEPTH, 3 * nx
    vmem = pl.BlockSpec(memory_space=pltpu.VMEM)
    params = pltpu.CompilerParams(vmem_limit_bytes=16 << 20)
    held, coef = pl.pallas_call(
        plane_kernel,
        out_shape=(jax.ShapeDtypeStruct(labels.shape, labels.dtype), jax.ShapeDtypeStruct((ROWS, nz), F32)),
        in_specs=[vmem] * 3,
        out_specs=(vmem, vmem),
        compiler_params=params,
    )(labels, layer_index.reshape(1, nz), layer_eps.reshape(1, -1))
    low, high = neighbours(labels, labels, "gx")
    centre = jnp.concatenate([low, held, high], 0)
    first, last = centre[:, :DEPTH], centre[:, ny - DEPTH :]
    second = lax.axis_index("gy") % 2 == 1
    left, right = neighbours(jnp.where(second, first, last), jnp.where(second, last, first), "gy")
    in_x, in_y = lax.axis_size("gx"), lax.axis_size("gy")
    early = pl.pallas_call(
        early_kernel,
        out_shape=[jax.ShapeDtypeStruct((rows, ny, ROWS, nz), F32)]
        + [jax.ShapeDtypeStruct((rows, ny, K, nz), F32)] * DEPTH,
        in_specs=[vmem] * 2,
        out_specs=[vmem] * (1 + DEPTH),
        compiler_params=params,
    )(centre, coef)
    field = pltpu.VMEM((rows, wide, K, nz), F32)
    parts, moments = pl.pallas_call(
        basis_kernel,
        out_shape=(
            jax.ShapeDtypeStruct((3 * DEPTH * K, nx * ny * nz), BF16),
            jax.ShapeDtypeStruct((in_y, ROWS, LANES), F32),
        ),
        in_specs=[vmem] * (4 + DEPTH),
        out_specs=(vmem, vmem),
        scratch_shapes=[pltpu.VMEM((rows, wide, ROWS, nz), F32)] + [field] * DEPTH,
        compiler_params=params,
    )(left, right, coef, *early)
    total = gathered(moments, "gy").sum(0)
    sums = gathered(jnp.broadcast_to(total[None], (in_x,) + total.shape), "gx")
    block = jax.ShapeDtypeStruct((K, nx, ny, nz), F32)
    return pl.pallas_call(
        outputs_kernel,
        out_shape=(block, block),
        in_specs=[vmem] * 3,
        out_specs=(vmem, vmem),
        scratch_shapes=[pltpu.VMEM((LANES, K), F32)],
        compiler_params=params,
    )(sums, parts, coef)


def solution(mesh):
    return jax.shard_map(
        on_device,
        mesh=mesh,
        in_specs=(P("gx", "gy", None), P(), P()),
        out_specs=(P(None, "gx", "gy", None), P(None, "gx", "gy", None)),
        check_vma=False,
    )
```

```python
import jax
import jax.numpy as jnp
from jax import lax
from jax.experimental import pallas as pl
from jax.experimental.pallas import tpu as pltpu
from jax.sharding import PartitionSpec as P

K = 16
STEPS = 3
DEPTH = STEPS + 1
ROWS = 8
LANES = 128
F32, BF16 = jnp.float32, jnp.bfloat16


def split(value):
    high = value.astype(BF16)
    rest = value - high.astype(F32)
    middle = rest.astype(BF16)
    return high, middle, (rest - middle.astype(F32)).astype(BF16)


def beyond(x, y, nx, ny):
    return max(nx - x, 0, x - 2 * nx + 1) + max(DEPTH - y, 0, y - DEPTH - ny + 1)


def is_early(level, x, y, nx, ny):
    return DEPTH + level <= y < DEPTH + ny - level and level <= x < 3 * nx - level


def excite(label, lateral_c):
    label = jnp.broadcast_to(label, lateral_c.shape)
    number = lax.broadcasted_iota(jnp.int32, lateral_c.shape, 0) + 1
    return (label == number).astype(F32), jnp.where(label == 0, lateral_c, 0.0)[:ROWS]


def next_power(x, y, power, factor, below_c, above_c):
    centre = power(x, y)
    lateral = (power(x - 1, y) + power(x + 1, y)) + (power(x, y - 1) + power(x, y + 1))
    last = centre.shape[1] - 1
    vertical = below_c * pltpu.roll(centre, 1, 1) + above_c * pltpu.roll(centre, last, 1)
    return jnp.concatenate([factor, factor], 0) * (lateral + vertical)


def early_kernel(centre_ref, coef_ref, weight, b0, b1, b2, b3):
    rows, ny, nz = centre_ref.shape
    nx = rows // 3
    lateral_c, below_c, above_c = (jnp.broadcast_to(coef_ref[i : i + 1, :], (K, nz)) for i in range(3))
    for x in range(rows):
        for y in range(ny):
            b0[x, y], weight[x, y] = excite(centre_ref[x, y : y + 1, :], lateral_c)
    powers = (b0, b1, b2, b3)
    for level in range(1, DEPTH):
        source = powers[level - 1]
        for x in range(rows):
            for y in range(ny):
                if is_early(level, x, y + DEPTH, nx, ny):
                    powers[level][x, y] = next_power(
                        x, y, lambda i, j, source=source: source[i, j], weight[x, y], below_c, above_c
                    )


def basis_kernel(left_ref, right_ref, coef_ref, early_weight, e0, e1, e2, e3, split_ref, moments_ref, weight, b0, b1, b2, b3):
    rows, ny, _, nz = early_weight.shape
    nx, wide = rows // 3, ny + 2 * DEPTH
    lateral_c, below_c, above_c, root = (jnp.broadcast_to(coef_ref[i : i + 1, :], (K, nz)) for i in range(4))
    for x in range(rows):
        for y in range(wide):
            if beyond(x, y, nx, ny) <= DEPTH and not is_early(0, x, y, nx, ny):
                ref, at = (left_ref, y) if y < DEPTH else (right_ref, y - DEPTH - ny)
                b0[x, y], weight[x, y] = excite(ref[x, at : at + 1, :], lateral_c)
    early, late = (e0, e1, e2, e3), (b0, b1, b2, b3)

    def power(level, x, y):
        return early[level][x, y - DEPTH] if is_early(level, x, y, nx, ny) else late[level][x, y]

    for level in range(1, DEPTH + 1):
        for x in range(rows):
            for y in range(wide):
                if beyond(x, y, nx, ny) > DEPTH - level:
                    continue
                if is_early(level, x, y, nx, ny):
                    value = power(level, x, y)
                else:
                    factor = early_weight[x, y - DEPTH] if is_early(0, x, y, nx, ny) else weight[x, y]
                    value = next_power(
                        x, y, lambda i, j, level=level: power(level - 1, i, j), factor, below_c, above_c
                    )
                    if level < DEPTH:
                        late[level][x, y] = value
                if beyond(x, y, nx, ny) == 0:
                    cell = (x - nx) * ny + y - DEPTH
                    for part, piece in enumerate(split(value * root)):
                        first = (part * DEPTH + level - 1) * K
                        split_ref[first : first + K, cell * nz : (cell + 1) * nz] = piece
    size, used = DEPTH * K, STEPS * K
    grams = lax.dot_general(
        jnp.concatenate([split_ref[part * size : part * size + used, :] for part in range(3)], 0),
        split_ref[...],
        (((1,), (1,)), ((), ())),
        preferred_element_type=F32,
    )

    def piece(i, j):
        return grams[i * used : (i + 1) * used, j * size : (j + 1) * size]

    gram = piece(0, 0) + ((piece(0, 1) + piece(1, 0)) + ((piece(0, 2) + piece(2, 0)) + piece(1, 1)))
    gram = jnp.concatenate([gram, jnp.zeros((used, LANES - size), F32)], 1)
    lane = lax.broadcasted_iota(jnp.int32, (K, LANES), 1)
    row = lax.broadcasted_iota(jnp.int32, (K, LANES), 0)
    packed = jnp.zeros((K, LANES), F32)
    for pair in range(3):
        start = pair * (K + 1)
        left, right = (pair + 3) // 2, pair // 2
        lower = pltpu.roll(gram[left * K : (left + 1) * K], (start - (pair + 4) // 2 * K) % LANES, 1)
        upper = pltpu.roll(gram[right * K : (right + 1) * K], (start + 1 - (pair + 1) // 2 * K) % LANES, 1)
        inside = (lane >= start) & (lane < start + K + 1)
        packed = jnp.where(inside, jnp.where(lane - start <= row, lower, upper), packed)
    folded = packed[:ROWS] + pltpu.roll(packed[ROWS:], LANES // 2, 1)
    for copy in range(moments_ref.shape[0]):
        moments_ref[copy] = folded


def eliminate(matrix):
    tiles = len(matrix)
    sub = lax.broadcasted_iota(jnp.int32, (ROWS, LANES), 0)
    for block in range(tiles):
        columns = [
            [
                jnp.broadcast_to(tile[:, block * ROWS + j : block * ROWS + j + 1], (ROWS, LANES))
                for tile in matrix
            ]
            for j in range(ROWS)
        ]
        for j in range(ROWS):
            column = columns[j]
            inverse = 1.0 / column[block][j : j + 1]
            line = matrix[block][j : j + 1] * inverse
            for later in range(j + 1, ROWS):
                other = columns[later]
                share = other[block][j : j + 1] * inverse
                columns[later] = [
                    jnp.where(sub == j, share, other[t] - column[t] * share) if t == block else other[t] - column[t] * share
                    for t in range(tiles)
                ]
            matrix = [
                jnp.where(sub == j, line, matrix[t] - column[t] * line) if t == block else matrix[t] - column[t] * line
                for t in range(tiles)
            ]
    return matrix


def outputs_kernel(parts_ref, split_ref, coef_ref, solution_out, residual_out, turned, solution_ref, residual_ref, sent):
    ny, nz = solution_ref.shape[2:]
    width = ny * nz
    sums = [parts_ref[part] for part in range(parts_ref.shape[0])]
    while len(sums) > 1:
        sums = [a + b for a, b in zip(sums[::2], sums[1::2])]
    folded = sums[0]
    packed = jnp.concatenate([folded, pltpu.roll(folded, LANES // 2, 1)], 0)
    turned[...] = packed.T
    lane = lax.broadcasted_iota(jnp.int32, (K, LANES), 1)
    row = lax.broadcasted_iota(jnp.int32, (K, LANES), 0)
    moments = jnp.zeros((K, LANES), F32)
    for power in range(2 * STEPS):
        pair, upper = power % 3, power < 3
        start = pair * (K + 1) + upper
        mirrored = jnp.concatenate([turned[start : start + K, :], jnp.zeros((K, LANES - K), F32)], 1)
        direct = pltpu.roll(packed, (power * K - start) % LANES, 1)
        mirrored = pltpu.roll(mirrored, power * K, 1) if power else mirrored
        column = lane - power * K
        chosen = jnp.where(column >= row, direct, mirrored) if upper else jnp.where(column <= row, direct, mirrored)
        moments = jnp.where((column >= 0) & (column < K), chosen, moments)
    images = moments - pltpu.roll(moments, LANES - K, 1)
    matrix = []
    for power in range(STEPS):
        left = images if power == 0 else pltpu.roll(images, LANES - power * K, 1)
        right = pltpu.roll(moments, (STEPS - power) * K, 1)
        block = jnp.where(lane < STEPS * K, left, right)
        matrix += [block[:ROWS], block[ROWS:]]
    matrix = jnp.concatenate(eliminate(matrix), 0)
    weights = matrix[:, STEPS * K : (STEPS + 1) * K].T
    first, second, third = weights[:, :K], weights[:, K : 2 * K], weights[:, 2 * K :]
    unit = (
        lax.broadcasted_iota(jnp.int32, (K, K), 0) == lax.broadcasted_iota(jnp.int32, (K, K), 1)
    ).astype(F32)
    none = jnp.zeros((K, K), F32)
    combine = jnp.concatenate(
        [
            jnp.concatenate([first, second, third, none], 1),
            jnp.concatenate([unit - first, first - second, second - third, third], 1),
        ],
        0,
    )
    high, middle, low = split(combine)
    zero = jnp.zeros(high.shape, BF16)
    factors = jnp.concatenate(
        [
            jnp.concatenate([high, high, high], 1),
            jnp.concatenate([middle, middle, zero], 1),
            jnp.concatenate([low, zero, zero], 1),
        ],
        0,
    )
    count = 2 * K
    root, over = coef_ref[3:4, :], coef_ref[4:5, :]
    copies = []
    for x in range(solution_ref.shape[1]):
        both = jnp.dot(factors, split_ref[:, x * width : (x + 1) * width], preferred_element_type=F32)
        both = both[:count] + (both[count : 2 * count] + both[2 * count :])
        for y in range(ny):
            block = both[:, y * nz : (y + 1) * nz]
            solution_ref[:, x, y, :] = block[:K] * over
            residual_ref[:, x, y, :] = block[K:] * root
        for i, (source, target) in enumerate(((solution_ref, solution_out), (residual_ref, residual_out))):
            copies.append(pltpu.make_async_copy(source.at[:, x], target.at[:, x], sent.at[i, x]))
            copies[-1].start()
    for copy in copies:
        copy.wait()


def plane_kernel(labels_ref, index_ref, eps_ref, held_ref, coef_ref):
    held_ref[...] = labels_ref[...]
    index = index_ref[...]
    eps = jnp.zeros(index.shape, F32)
    for layer in range(eps_ref.shape[1]):
        eps = jnp.where(index == layer, jnp.broadcast_to(eps_ref[:, layer : layer + 1], index.shape), eps)
    count = index.shape[1]
    lane = lax.broadcasted_iota(jnp.int32, index.shape, 1)
    down = jnp.where(lane == 0, eps, 0.5 * (eps + pltpu.roll(eps, 1, 1)))
    up = jnp.where(lane == count - 1, eps, 0.5 * (eps + pltpu.roll(eps, count - 1, 1)))
    diag = 4.0 * eps + down + up
    root = jnp.sqrt(diag)
    coef_ref[0:1, :] = eps / diag
    coef_ref[1:2, :] = jnp.where(lane == 0, 0.0, down / eps)
    coef_ref[2:3, :] = jnp.where(lane == count - 1, 0.0, up / eps)
    coef_ref[3:4, :] = root
    coef_ref[4:5, :] = 1.0 / root


def neighbours(to_even, to_odd, axis):
    count, at = lax.axis_size(axis), lax.axis_index(axis)
    pairs = [(i, i + 1) for i in range(1, count - 1, 2)]
    odd = lax.ppermute(to_odd, axis, pairs + [(j, i) for i, j in pairs])
    even = lax.ppermute(to_even, axis, [(i, i ^ 1) for i in range(count)])
    first = at % 2 == 0
    before = jnp.where(first, jnp.where(at > 0, odd, -1), even)
    after = jnp.where(first, even, jnp.where(at < count - 1, odd, -1))
    return before, after


def gathered(copies, axis):
    return lax.all_to_all(copies, axis, 0, 0, tiled=True)


def on_device(labels, layer_index, layer_eps):
    nx, ny, nz = labels.shape
    wide, rows = ny + 2 * DEPTH, 3 * nx
    vmem = pl.BlockSpec(memory_space=pltpu.VMEM)
    params = pltpu.CompilerParams(vmem_limit_bytes=16 << 20)
    held, coef = pl.pallas_call(
        plane_kernel,
        out_shape=(jax.ShapeDtypeStruct(labels.shape, labels.dtype), jax.ShapeDtypeStruct((ROWS, nz), F32)),
        in_specs=[vmem] * 3,
        out_specs=(vmem, vmem),
        compiler_params=params,
    )(labels, layer_index.reshape(1, nz), layer_eps.reshape(1, -1))
    low, high = neighbours(labels, labels, "gx")
    centre = jnp.concatenate([low, held, high], 0)
    first, last = centre[:, :DEPTH], centre[:, ny - DEPTH :]
    second = lax.axis_index("gy") % 2 == 1
    left, right = neighbours(jnp.where(second, first, last), jnp.where(second, last, first), "gy")
    in_x, in_y = lax.axis_size("gx"), lax.axis_size("gy")
    early = pl.pallas_call(
        early_kernel,
        out_shape=[jax.ShapeDtypeStruct((rows, ny, ROWS, nz), F32)]
        + [jax.ShapeDtypeStruct((rows, ny, K, nz), F32)] * DEPTH,
        in_specs=[vmem] * 2,
        out_specs=[vmem] * (1 + DEPTH),
        compiler_params=params,
    )(centre, coef)
    field = pltpu.VMEM((rows, wide, K, nz), F32)
    parts, moments = pl.pallas_call(
        basis_kernel,
        out_shape=(
            jax.ShapeDtypeStruct((3 * DEPTH * K, nx * ny * nz), BF16),
            jax.ShapeDtypeStruct((in_y, ROWS, LANES), F32),
        ),
        in_specs=[vmem] * (4 + DEPTH),
        out_specs=(vmem, vmem),
        scratch_shapes=[pltpu.VMEM((rows, wide, ROWS, nz), F32)] + [field] * DEPTH,
        compiler_params=params,
    )(left, right, coef, *early)
    total = gathered(moments, "gy").sum(0)
    sums = gathered(jnp.broadcast_to(total[None], (in_x,) + total.shape), "gx")
    block = jax.ShapeDtypeStruct((K, nx, ny, nz), F32)
    return pl.pallas_call(
        outputs_kernel,
        out_shape=(block, block),
        in_specs=[vmem] * 3,
        out_specs=(pl.BlockSpec(memory_space=pl.ANY),) * 2,
        scratch_shapes=[
            pltpu.VMEM((LANES, K), F32),
            pltpu.VMEM(block.shape, F32),
            pltpu.VMEM(block.shape, F32),
            pltpu.SemaphoreType.DMA((2, nx)),
        ],
        compiler_params=params,
    )(sums, parts, coef)


def solution(mesh):
    return jax.shard_map(
        on_device,
        mesh=mesh,
        in_specs=(P("gx", "gy", None), P(), P()),
        out_specs=(P(None, "gx", "gy", None), P(None, "gx", "gy", None)),
        check_vma=False,
    )
```

```python
import jax
import jax.numpy as jnp
from jax import lax
from jax.experimental import pallas as pl
from jax.experimental.pallas import tpu as pltpu
from jax.sharding import PartitionSpec as P

K = 16
STEPS = 3
DEPTH = STEPS + 1
ROWS = 8
LANES = 128
F32, BF16 = jnp.float32, jnp.bfloat16


def split(value):
    high = value.astype(BF16)
    rest = value - high.astype(F32)
    middle = rest.astype(BF16)
    return high, middle, (rest - middle.astype(F32)).astype(BF16)


def beyond(x, y, nx, ny):
    return max(nx - x, 0, x - 2 * nx + 1) + max(DEPTH - y, 0, y - DEPTH - ny + 1)


def is_early(level, x, y, nx, ny):
    return DEPTH + level <= y < DEPTH + ny - level and level <= x < 3 * nx - level


def excite(label, lateral_c):
    label = jnp.broadcast_to(label, lateral_c.shape)
    number = lax.broadcasted_iota(jnp.int32, lateral_c.shape, 0) + 1
    return (label == number).astype(F32), jnp.where(label == 0, lateral_c, 0.0)[:ROWS]


def next_power(x, y, power, factor, below_c, above_c):
    centre = power(x, y)
    lateral = (power(x - 1, y) + power(x + 1, y)) + (power(x, y - 1) + power(x, y + 1))
    last = centre.shape[1] - 1
    vertical = below_c * pltpu.roll(centre, 1, 1) + above_c * pltpu.roll(centre, last, 1)
    return jnp.concatenate([factor, factor], 0) * (lateral + vertical)


def early_kernel(centre_ref, coef_ref, weight, b0, b1, b2, b3):
    rows, ny, nz = centre_ref.shape
    nx = rows // 3
    lateral_c, below_c, above_c = (jnp.broadcast_to(coef_ref[i : i + 1, :], (K, nz)) for i in range(3))
    for x in range(rows):
        for y in range(ny):
            b0[x, y], weight[x, y] = excite(centre_ref[x, y : y + 1, :], lateral_c)
    powers = (b0, b1, b2, b3)
    for level in range(1, DEPTH):
        source = powers[level - 1]
        for x in range(rows):
            for y in range(ny):
                if is_early(level, x, y + DEPTH, nx, ny):
                    powers[level][x, y] = next_power(
                        x, y, lambda i, j, source=source: source[i, j], weight[x, y], below_c, above_c
                    )


def basis_kernel(left_ref, right_ref, coef_ref, early_weight, e0, e1, e2, e3, split_ref, moments_ref, weight, b0, b1, b2, b3):
    rows, ny, _, nz = early_weight.shape
    nx, wide = rows // 3, ny + 2 * DEPTH
    lateral_c, below_c, above_c, root = (jnp.broadcast_to(coef_ref[i : i + 1, :], (K, nz)) for i in range(4))
    for x in range(rows):
        for y in range(wide):
            if beyond(x, y, nx, ny) <= DEPTH and not is_early(0, x, y, nx, ny):
                ref, at = (left_ref, y) if y < DEPTH else (right_ref, y - DEPTH - ny)
                b0[x, y], weight[x, y] = excite(ref[x, at : at + 1, :], lateral_c)
    early, late = (e0, e1, e2, e3), (b0, b1, b2, b3)

    def power(level, x, y):
        return early[level][x, y - DEPTH] if is_early(level, x, y, nx, ny) else late[level][x, y]

    for level in range(1, DEPTH + 1):
        for x in range(rows):
            for y in range(wide):
                if beyond(x, y, nx, ny) > DEPTH - level:
                    continue
                if is_early(level, x, y, nx, ny):
                    value = power(level, x, y)
                else:
                    factor = early_weight[x, y - DEPTH] if is_early(0, x, y, nx, ny) else weight[x, y]
                    value = next_power(
                        x, y, lambda i, j, level=level: power(level - 1, i, j), factor, below_c, above_c
                    )
                    if level < DEPTH:
                        late[level][x, y] = value
                if beyond(x, y, nx, ny) == 0:
                    cell = (x - nx) * ny + y - DEPTH
                    for part, piece in enumerate(split(value * root)):
                        first = (part * DEPTH + level - 1) * K
                        split_ref[first : first + K, cell * nz : (cell + 1) * nz] = piece
    size, used = DEPTH * K, STEPS * K
    grams = lax.dot_general(
        jnp.concatenate([split_ref[part * size : part * size + used, :] for part in range(3)], 0),
        split_ref[...],
        (((1,), (1,)), ((), ())),
        preferred_element_type=F32,
    )

    def piece(i, j):
        return grams[i * used : (i + 1) * used, j * size : (j + 1) * size]

    gram = piece(0, 0) + ((piece(0, 1) + piece(1, 0)) + ((piece(0, 2) + piece(2, 0)) + piece(1, 1)))
    gram = jnp.concatenate([gram, jnp.zeros((used, LANES - size), F32)], 1)
    lane = lax.broadcasted_iota(jnp.int32, (K, LANES), 1)
    row = lax.broadcasted_iota(jnp.int32, (K, LANES), 0)
    packed = jnp.zeros((K, LANES), F32)
    for pair in range(3):
        start = pair * (K + 1)
        left, right = (pair + 3) // 2, pair // 2
        lower = pltpu.roll(gram[left * K : (left + 1) * K], (start - (pair + 4) // 2 * K) % LANES, 1)
        upper = pltpu.roll(gram[right * K : (right + 1) * K], (start + 1 - (pair + 1) // 2 * K) % LANES, 1)
        inside = (lane >= start) & (lane < start + K + 1)
        packed = jnp.where(inside, jnp.where(lane - start <= row, lower, upper), packed)
    folded = packed[:ROWS] + pltpu.roll(packed[ROWS:], LANES // 2, 1)
    for copy in range(moments_ref.shape[0]):
        moments_ref[copy] = folded


def eliminate(matrix):
    tiles = len(matrix)
    sub = lax.broadcasted_iota(jnp.int32, (ROWS, LANES), 0)

    def column_of(tile, at):
        return jnp.broadcast_to(tile[:, at : at + 1], (ROWS, LANES))

    for block in range(tiles):
        below = range(block, tiles)
        columns = [{t: column_of(matrix[t], block * ROWS + j) for t in below} for j in range(ROWS)]
        matrix = list(matrix)
        for j in range(ROWS):
            column = columns[j]
            inverse = 1.0 / column[block][j : j + 1]
            line = matrix[block][j : j + 1] * inverse
            for later in range(j + 1, ROWS):
                other = columns[later]
                share = other[block][j : j + 1] * inverse
                columns[later] = {t: other[t] - column[t] * share for t in below}
                columns[later][block] = jnp.where(sub == j, share, columns[later][block])
            for t in below:
                cleared = matrix[t] - column[t] * line
                matrix[t] = jnp.where(sub == j, line, cleared) if t == block else cleared
    for block in reversed(range(tiles - 1)):
        terms = [
            column_of(matrix[block], t * ROWS + j) * matrix[t][j : j + 1]
            for t in range(block + 1, tiles)
            for j in range(ROWS)
        ]
        while len(terms) > 1:
            terms = [x + y for x, y in zip(terms[::2], terms[1::2])] + ([terms[-1]] if len(terms) % 2 else [])
        matrix[block] = matrix[block] - terms[0]
    return matrix


def outputs_kernel(parts_ref, split_ref, coef_ref, solution_out, residual_out, turned, solution_ref, residual_ref, sent):
    ny, nz = solution_ref.shape[2:]
    width = ny * nz
    sums = [parts_ref[part] for part in range(parts_ref.shape[0])]
    while len(sums) > 1:
        sums = [a + b for a, b in zip(sums[::2], sums[1::2])]
    folded = sums[0]
    packed = jnp.concatenate([folded, pltpu.roll(folded, LANES // 2, 1)], 0)
    turned[...] = packed.T
    lane = lax.broadcasted_iota(jnp.int32, (K, LANES), 1)
    row = lax.broadcasted_iota(jnp.int32, (K, LANES), 0)
    moments = jnp.zeros((K, LANES), F32)
    for power in range(2 * STEPS):
        pair, upper = power % 3, power < 3
        start = pair * (K + 1) + upper
        mirrored = jnp.concatenate([turned[start : start + K, :], jnp.zeros((K, LANES - K), F32)], 1)
        direct = pltpu.roll(packed, (power * K - start) % LANES, 1)
        mirrored = pltpu.roll(mirrored, power * K, 1) if power else mirrored
        column = lane - power * K
        chosen = jnp.where(column >= row, direct, mirrored) if upper else jnp.where(column <= row, direct, mirrored)
        moments = jnp.where((column >= 0) & (column < K), chosen, moments)
    images = moments - pltpu.roll(moments, LANES - K, 1)
    matrix = []
    for power in range(STEPS):
        left = images if power == 0 else pltpu.roll(images, LANES - power * K, 1)
        right = pltpu.roll(moments, (STEPS - power) * K, 1)
        block = jnp.where(lane < STEPS * K, left, right)
        matrix += [block[:ROWS], block[ROWS:]]
    matrix = jnp.concatenate(eliminate(matrix), 0)
    weights = matrix[:, STEPS * K : (STEPS + 1) * K].T
    first, second, third = weights[:, :K], weights[:, K : 2 * K], weights[:, 2 * K :]
    unit = (
        lax.broadcasted_iota(jnp.int32, (K, K), 0) == lax.broadcasted_iota(jnp.int32, (K, K), 1)
    ).astype(F32)
    none = jnp.zeros((K, K), F32)
    combine = jnp.concatenate(
        [
            jnp.concatenate([first, second, third, none], 1),
            jnp.concatenate([unit - first, first - second, second - third, third], 1),
        ],
        0,
    )
    high, middle, low = split(combine)
    zero = jnp.zeros(high.shape, BF16)
    factors = jnp.concatenate(
        [
            jnp.concatenate([high, high, high], 1),
            jnp.concatenate([middle, middle, zero], 1),
            jnp.concatenate([low, zero, zero], 1),
        ],
        0,
    )
    count = 2 * K
    root, over = coef_ref[3:4, :], coef_ref[4:5, :]
    copies = []
    for x in range(solution_ref.shape[1]):
        both = jnp.dot(factors, split_ref[:, x * width : (x + 1) * width], preferred_element_type=F32)
        both = both[:count] + (both[count : 2 * count] + both[2 * count :])
        for y in range(ny):
            block = both[:, y * nz : (y + 1) * nz]
            solution_ref[:, x, y, :] = block[:K] * over
            residual_ref[:, x, y, :] = block[K:] * root
        for i, (source, target) in enumerate(((solution_ref, solution_out), (residual_ref, residual_out))):
            copies.append(pltpu.make_async_copy(source.at[:, x], target.at[:, x], sent.at[i, x]))
            copies[-1].start()
    for copy in copies:
        copy.wait()


def plane_kernel(labels_ref, index_ref, eps_ref, held_ref, coef_ref):
    held_ref[...] = labels_ref[...]
    index = index_ref[...]
    eps = jnp.zeros(index.shape, F32)
    for layer in range(eps_ref.shape[1]):
        eps = jnp.where(index == layer, jnp.broadcast_to(eps_ref[:, layer : layer + 1], index.shape), eps)
    count = index.shape[1]
    lane = lax.broadcasted_iota(jnp.int32, index.shape, 1)
    down = jnp.where(lane == 0, eps, 0.5 * (eps + pltpu.roll(eps, 1, 1)))
    up = jnp.where(lane == count - 1, eps, 0.5 * (eps + pltpu.roll(eps, count - 1, 1)))
    diag = 4.0 * eps + down + up
    root = jnp.sqrt(diag)
    coef_ref[0:1, :] = eps / diag
    coef_ref[1:2, :] = jnp.where(lane == 0, 0.0, down / eps)
    coef_ref[2:3, :] = jnp.where(lane == count - 1, 0.0, up / eps)
    coef_ref[3:4, :] = root
    coef_ref[4:5, :] = 1.0 / root


def neighbours(to_even, to_odd, axis):
    count, at = lax.axis_size(axis), lax.axis_index(axis)
    pairs = [(i, i + 1) for i in range(1, count - 1, 2)]
    odd = lax.ppermute(to_odd, axis, pairs + [(j, i) for i, j in pairs])
    even = lax.ppermute(to_even, axis, [(i, i ^ 1) for i in range(count)])
    first = at % 2 == 0
    before = jnp.where(first, jnp.where(at > 0, odd, -1), even)
    after = jnp.where(first, even, jnp.where(at < count - 1, odd, -1))
    return before, after


def gathered(copies, axis):
    return lax.all_to_all(copies, axis, 0, 0, tiled=True)


def on_device(labels, layer_index, layer_eps):
    nx, ny, nz = labels.shape
    wide, rows = ny + 2 * DEPTH, 3 * nx
    vmem = pl.BlockSpec(memory_space=pltpu.VMEM)
    params = pltpu.CompilerParams(vmem_limit_bytes=16 << 20)
    held, coef = pl.pallas_call(
        plane_kernel,
        out_shape=(jax.ShapeDtypeStruct(labels.shape, labels.dtype), jax.ShapeDtypeStruct((ROWS, nz), F32)),
        in_specs=[vmem] * 3,
        out_specs=(vmem, vmem),
        compiler_params=params,
    )(labels, layer_index.reshape(1, nz), layer_eps.reshape(1, -1))
    low, high = neighbours(labels, labels, "gx")
    centre = jnp.concatenate([low, held, high], 0)
    first, last = centre[:, :DEPTH], centre[:, ny - DEPTH :]
    second = lax.axis_index("gy") % 2 == 1
    left, right = neighbours(jnp.where(second, first, last), jnp.where(second, last, first), "gy")
    in_x, in_y = lax.axis_size("gx"), lax.axis_size("gy")
    early = pl.pallas_call(
        early_kernel,
        out_shape=[jax.ShapeDtypeStruct((rows, ny, ROWS, nz), F32)]
        + [jax.ShapeDtypeStruct((rows, ny, K, nz), F32)] * DEPTH,
        in_specs=[vmem] * 2,
        out_specs=[vmem] * (1 + DEPTH),
        compiler_params=params,
    )(centre, coef)
    field = pltpu.VMEM((rows, wide, K, nz), F32)
    parts, moments = pl.pallas_call(
        basis_kernel,
        out_shape=(
            jax.ShapeDtypeStruct((3 * DEPTH * K, nx * ny * nz), BF16),
            jax.ShapeDtypeStruct((in_y, ROWS, LANES), F32),
        ),
        in_specs=[vmem] * (4 + DEPTH),
        out_specs=(vmem, vmem),
        scratch_shapes=[pltpu.VMEM((rows, wide, ROWS, nz), F32)] + [field] * DEPTH,
        compiler_params=params,
    )(left, right, coef, *early)
    total = gathered(moments, "gy").sum(0)
    sums = gathered(jnp.broadcast_to(total[None], (in_x,) + total.shape), "gx")
    block = jax.ShapeDtypeStruct((K, nx, ny, nz), F32)
    return pl.pallas_call(
        outputs_kernel,
        out_shape=(block, block),
        in_specs=[vmem] * 3,
        out_specs=(pl.BlockSpec(memory_space=pl.ANY),) * 2,
        scratch_shapes=[
            pltpu.VMEM((LANES, K), F32),
            pltpu.VMEM(block.shape, F32),
            pltpu.VMEM(block.shape, F32),
            pltpu.SemaphoreType.DMA((2, nx)),
        ],
        compiler_params=params,
    )(sums, parts, coef)


def solution(mesh):
    return jax.shard_map(
        on_device,
        mesh=mesh,
        in_specs=(P("gx", "gy", None), P(), P()),
        out_specs=(P(None, "gx", "gy", None), P(None, "gx", "gy", None)),
        check_vma=False,
    )
```
